512 devices in a mesh: mesh: 64 (over x, y, z_lo), state: 8 (over z_hi, core).
Axes of the slice: x: 4, y: 8, z: 8 (z_hi: 4, z_lo: 2; z = z_hi * 2 + z_lo), core: 2. Of those that a mesh axis runs over, the one named last changes fastest.
Arguments:
- subspace: float32 [2048, 16384], P('state', 'mesh'), may hold values from -6 to 6
- ritz: float32 [1024, 2048], P('state'), may hold values from -0.125 to 0.125
- element_ham: float32 [1024, 125, 125], P('mesh'), may hold values from -0.6 to 0.6
- connect: int32 [1024, 125], P('mesh'), may hold values from 0 to 383, as said below
- send_rows: int32 [64, 4, 32], P('mesh'), may hold values from 0 to 255, as said below
Outputs:
- filtered: float32 [1024, 16384], P('state', 'mesh')
The draws below stay inside these ranges and needn't reach their ends.
Inputs may be any that keep to these rules, and one draw needn't show every extreme that they name: send_rows[p][k] lists nodes of partition p, local numbering, that neighbour k of p uses; only a leading part of each list, of 32 entries or fewer, is used, and some partition uses a whole list. `connect`: entries below 256 are the partition's own nodes; an entry 256 + k * 32 + j is entry j of the list that neighbour k keeps for this partition.
All inputs are finite; a program needn't handle non-finite values.
Results may differ from the reference program's by a relative error of at most 0.0001.
Values sent between devices are 32-bit elements; how exact they have to be, the bound alone decides.
A program may use at most 64 MiB of HBM per device.

```python
import jax
import jax.numpy as jnp
from jax import lax

STATES = 2048
BLOCK = 1024
ELEM_NODES = 125
NODE_DEV = 256
ELEM_DEV = 16
HALO = 32
NODES = 16384
ELEMS = 1024
N_MESH = 64


def topology(key):
    base = jax.random.fold_in(key, 11)
    keys = jax.random.split(base, 3)
    across = N_MESH // 2
    offsets = jnp.array([1, -1, across, -across], jnp.int32)
    partition = jnp.arange(N_MESH, dtype=jnp.int32)
    neighbour_ids = (partition[:, None] + offsets[None, :] + N_MESH) % N_MESH
    lowest = max(1, HALO // 4)
    counts = jax.random.randint(keys[1], (N_MESH, 4), lowest, HALO + 1)
    chosen = jax.random.randint(keys[2], (), 0, N_MESH)
    counts = counts.at[chosen, 2].set(HALO)
    return (neighbour_ids.astype(jnp.int32), counts, chosen)


def draw_send_rows(key, part):
    return jax.random.randint(jax.random.fold_in(key, 13), (N_MESH, 4, HALO), 0, NODE_DEV).astype(jnp.int32)


def draw_connect(key, part):
    neighbour_ids, counts, chosen = topology(key)
    reverse = jnp.array([1, 0, 3, 2], jnp.int32)
    incoming = counts[neighbour_ids, reverse[None, :]]
    keys = jax.random.split(jax.random.fold_in(key, 17), 4)
    total_rows = ELEM_DEV * N_MESH
    shape = (total_rows, ELEM_NODES)
    device = jnp.arange(total_rows, dtype=jnp.int32) // ELEM_DEV
    ghost = jax.random.randint(keys[0], shape, 0, 4) == 0
    slot_index = jax.random.randint(keys[1], shape, 0, 4)
    spread = jax.random.randint(keys[2], shape, 0, 1 << 20)
    limit = incoming[device[:, None], slot_index]
    place = spread % limit
    own_rows = jax.random.randint(keys[3], shape, 0, NODE_DEV)
    result = jnp.where(ghost, NODE_DEV + slot_index * HALO + place, own_rows)
    target = neighbour_ids[chosen, 2]
    result = result.at[target * ELEM_DEV, 0].set(NODE_DEV + 4 * HALO - 1)
    return result.astype(jnp.int32)


def levels(own_key, dims, cuts, smallest, high):
    level, own = 1.0, jax.random.fold_in(own_key, 6)
    for position, blocks in cuts:
        heights = jnp.exp(jax.random.uniform(jax.random.fold_in(own, position), (blocks,), jnp.float32, smallest / len(cuts), high / len(cuts)))
        level = level * jnp.repeat(heights, dims[position] // blocks).reshape([-1 if axis == position else 1 for axis in range(len(dims))])
    return level


def noise(key, extent, width, bound, shards=(), kind=jnp.bfloat16):
    drawn = jax.random.normal(key, extent, jnp.float32) * width
    if len(shards) > 0:
        drawn = levels(key, extent, shards, -0.22, 0.18) * drawn
    return jnp.clip(drawn, min=-bound, max=bound).astype(kind)


def setup_inputs(seed: int = 0) -> dict:
    key_list = jax.random.split(jax.random.key(seed), 6)
    subspace = noise(key_list[0], (STATES, NODES), 1.0, 6.0, ((0, 8), (1, 64)), jnp.float32)
    ritz = noise(key_list[1], (BLOCK, STATES), STATES ** -0.5, 0.125, ((0, 8),), jnp.float32)
    element_ham = noise(key_list[2], (ELEMS, ELEM_NODES, ELEM_NODES), 0.1, 0.6, ((0, 64),), jnp.float32)
    connect = draw_connect(jax.random.fold_in(key_list[5], 71), 0)
    send_rows = draw_send_rows(jax.random.fold_in(key_list[5], 71), 0)
    return dict(subspace=subspace, ritz=ritz, element_ham=element_ham, connect=connect, send_rows=send_rows)


def global_connect(connect, send_rows):
    grouped = connect.reshape(N_MESH, ELEM_DEV, ELEM_NODES).astype(jnp.int32)
    partition = jnp.arange(N_MESH, dtype=jnp.int32)[:, None, None]
    across = N_MESH // 2
    offsets = jnp.array([1, -1, across, -across], jnp.int32)
    offset = jnp.maximum(grouped - NODE_DEV, 0)
    slot_index = offset // HALO
    place = offset % HALO
    owner = (partition + offsets[slot_index] + N_MESH) % N_MESH
    back_slot = slot_index + 1 - 2 * (slot_index % 2)
    remote = owner * NODE_DEV + send_rows[owner, back_slot, place]
    return jnp.where(grouped < NODE_DEV, partition * NODE_DEV + grouped, remote).astype(jnp.int32)


def apply_ham(vectors, node_table, element_ham):
    hams = element_ham.reshape(N_MESH, ELEM_DEV, ELEM_NODES, ELEM_NODES)

    def visit(result, item):
        indices, matrices = item
        gathered = vectors[:, indices]
        product = jnp.einsum('eab,ceb->cea', matrices, gathered, precision=lax.Precision.HIGHEST)
        return result.at[:, indices].add(product), None

    result, _ = lax.scan(visit, jnp.zeros_like(vectors), (node_table, hams))
    return result


def reference(subspace, ritz, element_ham, connect, send_rows):
    node_table = global_connect(connect, send_rows)
    half = 1.5
    centre = 2.5
    sigma_one = half / (-1.0 - centre)
    sigma_two = 1.0 / (2.0 / sigma_one - sigma_one)
    start_block = jnp.dot(ritz, subspace, precision=lax.Precision.HIGHEST, preferred_element_type=jnp.float32)
    first = (sigma_one / half) * (apply_ham(start_block, node_table, element_ham) - centre * start_block)
    second = (2.0 * sigma_two / half) * (apply_ham(first, node_table, element_ham) - centre * first)
    return second - sigma_one * sigma_two * start_block
```

```python
import functools

import jax
import jax.numpy as jnp
from jax import lax
from jax.experimental import pallas as pl
from jax.experimental.pallas import tpu as pltpu
from jax.sharding import PartitionSpec as P

MESH = pl.DeviceIdType.MESH
F32 = jnp.float32
BF16 = jnp.bfloat16
PIECES = 4


def split(value):
    high = value.astype(BF16)
    low = (value - high.astype(F32)).astype(BF16)
    return high, low


def dot(left, right):
    return jnp.dot(left, right, preferred_element_type=F32)


def dot_nt(left, right):
    return lax.dot_general(
        left, right, (((1,), (1,)), ((), ())), preferred_element_type=F32
    )


def left3(value):
    high, low = split(value)
    return jnp.concatenate([high, low, high], axis=1)


def right3(value, axis):
    high, low = split(value)
    return jnp.concatenate([high, high, low], axis=axis)


def right2(value, axis):
    high, low = split(value)
    return jnp.concatenate([high, low], axis=axis)


def kernel(
    n_mesh,
    sub_hbm,
    ritz_hbm,
    ham_hbm,
    connect_hbm,
    rows_hbm,
    out_ref,
    gathered,
    ritz_in,
    ritz_cat,
    ham_in,
    ham_pad,
    connect_in,
    connect_pad,
    rows_in,
    op_sum,
    op_cat,
    op_gg,
    op_og,
    start_acc,
    sends,
    takes,
    local_sem,
    ag_send,
    ag_recv,
    halo_send,
    halo_recv,
):
    own_part = lax.axis_index("mesh")
    state = lax.axis_index("state")
    core = lax.rem(state, 2)
    sibling = state + 1 - 2 * core
    right = lax.rem(state + 2, 8)
    left = lax.rem(state + 6, 8)
    across = lax.rem(state + 4, 8)
    above = lax.rem(own_part + 1, n_mesh)
    below = lax.rem(own_part + n_mesh - 1, n_mesh)
    far = lax.rem(own_part + n_mesh // 2, n_mesh)

    barrier = pltpu.get_barrier_semaphore()
    for peer in (sibling, right, left):
        pl.semaphore_signal(
            barrier, inc=1, device_id={"state": peer}, device_id_type=MESH
        )
    for peer in (above, below, far):
        pl.semaphore_signal(
            barrier, inc=1, device_id={"mesh": peer}, device_id_type=MESH
        )

    loads = [
        pltpu.make_async_copy(connect_hbm, connect_in, local_sem.at[0]),
        pltpu.make_async_copy(rows_hbm, rows_in, local_sem.at[1]),
        pltpu.make_async_copy(ham_hbm, ham_in, local_sem.at[2]),
        pltpu.make_async_copy(sub_hbm, gathered.at[state], local_sem.at[3]),
        pltpu.make_async_copy(ritz_hbm, ritz_in, local_sem.at[4]),
    ]
    for load in loads:
        load.start()
    pl.semaphore_wait(barrier, 6)

    n = PIECES
    size = 256 // n
    half = n // 2

    def transfer(source, target, number, peer):
        return pltpu.make_async_remote_copy(
            src_ref=source,
            dst_ref=target,
            send_sem=ag_send.at[number],
            recv_sem=ag_recv.at[number],
            device_id={"state": peer},
            device_id_type=MESH,
        )

    def piece(owner, i):
        return gathered.at[owner, pl.ds(i * size, size)]

    def own_piece(i):
        return sub_hbm.at[pl.ds(i * size, size)]

    def to_right(i, source, owner):
        return transfer(source, piece(owner, i), i, right)

    def to_left(i, source, owner):
        return transfer(source, piece(owner, i), n + i, left)

    def on_right(i, owner):
        return transfer(piece(owner, i), piece(owner, i), 2 * n + i, right)

    def on_left(i, owner):
        return transfer(piece(owner, i), piece(owner, i), 2 * n + i, left)

    def to_sibling(i, base, owner):
        return transfer(
            piece(owner, i), piece(owner, i), (3 + base) * n + i, sibling
        )

    own_sibling = transfer(sub_hbm, gathered.at[state], 6 * n, sibling)
    started = [own_sibling]
    lows = list(range(half))
    highs = list(range(half, n))
    order = list(zip(lows + highs, highs + lows))
    for i, j in order:
        a = to_right(i, own_piece(i), state)
        b = to_left(j, own_piece(j), state)
        a.start()
        b.start()
        started += [a, b]
        if i == 0:
            own_sibling.start()

    loads[0].wait()
    loads[1].wait()
    connect_pad[...] = jnp.full((16, 128), -1, jnp.int32)
    connect_pad[:, 0:125] = connect_in[...]
    ham_pad[...] = jnp.zeros((16, 128, 128), F32)
    loads[2].wait()
    ham_pad[:, 0:125, 0:125] = ham_in[...]
    op_sum[...] = jnp.zeros((384, 384), F32)

    def assemble(e, carry):
        names = connect_pad[pl.ds(e, 1), :]
        names = jnp.where(
            names >= 352, names - 32, jnp.where(names >= 320, names + 32, names)
        )
        pick = (
            lax.broadcasted_iota(jnp.int32, (384, 128), 0) == names
        ).astype(F32).astype(BF16)
        high, low = split(ham_pad[e])
        pick2 = jnp.concatenate([pick, pick], axis=1)
        spread = dot_nt(jnp.concatenate([high, low], axis=1), pick2)
        op_sum[...] += dot(pick2, right2(spread, 0))
        return carry

    lax.fori_loop(0, 16, assemble, 0)

    send_names = jnp.concatenate(
        [rows_in[0, pl.ds(k, 1), :] for k in range(4)], axis=1
    )
    place_f = (
        lax.broadcasted_iota(jnp.int32, (256, 128), 0) == send_names
    ).astype(F32)
    place = place_f.astype(BF16)
    take = jnp.transpose(place_f).astype(BF16)
    take2 = jnp.concatenate([take, take], axis=1)
    place2 = jnp.concatenate([place, place], axis=1)
    same = dot(take, place).astype(BF16)
    same2 = jnp.concatenate([same, same], axis=1)
    take_rows2 = jnp.concatenate([take, take], axis=0)

    centre = 2.5
    eye = (
        lax.broadcasted_iota(jnp.int32, (384, 256), 0)
        == lax.broadcasted_iota(jnp.int32, (384, 256), 1)
    ).astype(F32)
    op_cat[...] = left3(op_sum[:, 0:256] - centre * eye)
    ghost_cols = left3(op_sum[:, 256:384])
    op_og[...] = ghost_cols[0:256]
    op_gg[...] = ghost_cols[256:384]

    loads[4].wait()
    for i in range(16):
        ritz_cat[i] = left3(ritz_in[:, 128 * i : 128 * i + 128])

    def rotate(owner, h):
        block = gathered[owner, 128 * h : 128 * h + 128, :]
        start_acc[...] += dot(ritz_cat[2 * owner + h], right3(block, 0))

    start_acc[...] = jnp.zeros((128, 256), F32)
    loads[3].wait()
    rotate(state, 0)
    rotate(state, 1)

    def pass_on(copies):
        for copy in copies:
            copy.start()
        started.extend(copies)

    for i, j in zip(lows, highs):
        to_right(i, piece(left, i), left).wait_recv()
        pass_on([on_right(i, left), to_sibling(i, 0, left)])
        to_left(j, piece(right, j), right).wait_recv()
        pass_on([on_left(j, right), to_sibling(j, 1, right)])
    transfer(gathered.at[sibling], gathered.at[sibling], 6 * n, sibling).wait_recv()
    rotate(sibling, 0)
    rotate(sibling, 1)
    rotate(left, 0)
    rotate(right, 1)
    for i, j in zip(highs, lows):
        to_right(i, piece(left, i), left).wait_recv()
        pass_on([to_sibling(i, 0, left)])
        to_left(j, piece(right, j), right).wait_recv()
        pass_on([to_sibling(j, 1, right)])
    rotate(left, 1)
    rotate(right, 0)
    other_left = lax.rem(sibling + 6, 8)
    other_right = lax.rem(sibling + 2, 8)
    other_across = lax.rem(sibling + 4, 8)
    for i, j in zip(lows, highs):
        on_right(i, across).wait_recv()
        pass_on([to_sibling(i, 2, across)])
        on_left(j, across).wait_recv()
        pass_on([to_sibling(j, 2, across)])
    for h, pieces in ((0, lows), (1, highs)):
        for i in pieces:
            to_sibling(i, 0, other_left).wait_recv()
        rotate(other_left, h)
        for i in pieces:
            to_sibling(i, 1, other_right).wait_recv()
        rotate(other_right, h)
    rotate(across, 0)
    rotate(across, 1)
    for h, pieces in ((0, lows), (1, highs)):
        for i in pieces:
            to_sibling(i, 2, other_across).wait_recv()
        rotate(other_across, h)

    start = start_acc[...]

    def exchange(number):
        copies = []
        for k, (first, count, target, peer) in enumerate(
            ((0, 32, 32, above), (32, 32, 0, below), (64, 64, 64, far))
        ):
            copies.append(
                pltpu.make_async_remote_copy(
                    src_ref=sends.at[number, pl.ds(first, count)],
                    dst_ref=takes.at[number, pl.ds(target, count)],
                    send_sem=halo_send.at[number, k],
                    recv_sem=halo_recv.at[number, k],
                    device_id={"mesh": peer},
                    device_id_type=MESH,
                )
            )
        for copy in copies:
            copy.start()
        started.extend(copies)
        return copies

    def arrive(copies):
        for copy in copies:
            copy.wait_recv()
        return takes[len(halos) - 1]

    sigma_one = 1.5 / (-1.0 - centre)
    sigma_two = 1.0 / (2.0 / sigma_one - sigma_one)
    scale_one = sigma_one / 1.5
    scale_two = 2.0 * sigma_two / 1.5
    halos = []

    sends[0] = dot_nt(take2, right2(start, 1))
    halos.append(exchange(0))
    base = dot_nt(op_cat[...], right3(start, 1))
    ghosts = right3(arrive(halos[0]), 0)
    sends[1] = base[256:384] + dot(op_gg[...], ghosts)
    halos.append(exchange(1))
    own = base[0:256] + dot(op_og[...], ghosts)
    own_packed = dot(take2, right2(own, 0))
    back = right2(arrive(halos[1]), 0)
    sends[2] = scale_one * (own_packed + dot(same2, back))
    halos.append(exchange(2))
    first = scale_one * (own + dot(place2, back))
    base = dot(op_cat[...], right3(first, 0))
    ghosts = right3(arrive(halos[2]), 0)
    sends[3] = base[256:384] + dot(op_gg[...], ghosts)
    halos.append(exchange(3))
    own = base[0:256] + dot(op_og[...], ghosts)
    rest = scale_two * jnp.transpose(own) - sigma_one * sigma_two * start
    back = right2(jnp.transpose(arrive(halos[3])), 1)
    out_ref[...] = rest + scale_two * dot(back, take_rows2)

    for copy in started:
        copy.wait_send()


def solution(mesh):
    n_mesh = mesh.shape["mesh"]

    def per_device(subspace, ritz, element_ham, connect, send_rows):
        any_space = pl.BlockSpec(memory_space=pl.ANY)
        copies = 6 * PIECES + 1
        return pl.pallas_call(
            functools.partial(kernel, n_mesh),
            out_shape=jax.ShapeDtypeStruct((128, 256), F32),
            in_specs=[any_space] * 5,
            out_specs=pl.BlockSpec(memory_space=pltpu.VMEM),
            scratch_shapes=[
                pltpu.VMEM((8, 256, 256), F32),
                pltpu.VMEM((128, 2048), F32),
                pltpu.VMEM((16, 128, 384), BF16),
                pltpu.VMEM((16, 125, 125), F32),
                pltpu.VMEM((16, 128, 128), F32),
                pltpu.VMEM((16, 125), jnp.int32),
                pltpu.VMEM((16, 128), jnp.int32),
                pltpu.VMEM((1, 4, 32), jnp.int32),
                pltpu.VMEM((384, 384), F32),
                pltpu.VMEM((384, 768), BF16),
                pltpu.VMEM((128, 384), BF16),
                pltpu.VMEM((256, 384), BF16),
                pltpu.VMEM((128, 256), F32),
                pltpu.VMEM((4, 128, 128), F32),
                pltpu.VMEM((4, 128, 128), F32),
                pltpu.SemaphoreType.DMA((5,)),
                pltpu.SemaphoreType.DMA((copies,)),
                pltpu.SemaphoreType.DMA((copies,)),
                pltpu.SemaphoreType.DMA((4, 3)),
                pltpu.SemaphoreType.DMA((4, 3)),
            ],
            compiler_params=pltpu.CompilerParams(
                collective_id=0,
                has_side_effects=True,
                vmem_limit_bytes=40 * 1024 * 1024,
            ),
        )(subspace, ritz, element_ham, connect, send_rows)

    return jax.shard_map(
        per_device,
        mesh=mesh,
        in_specs=(
            P("state", "mesh"),
            P("state", None),
            P("mesh", None, None),
            P("mesh", None),
            P("mesh", None, None),
        ),
        out_specs=P("state", "mesh"),
        check_vma=False,
    )
```

```python
import functools

import jax
import jax.numpy as jnp
from jax import lax
from jax.experimental import pallas as pl
from jax.experimental.pallas import tpu as pltpu
from jax.sharding import PartitionSpec as P

MESH = pl.DeviceIdType.MESH
F32 = jnp.float32
BF16 = jnp.bfloat16
PIECES = 8
SIDE = PIECES // 2
SIZE = 256 // PIECES


def split(value):
    high = value.astype(BF16)
    low = (value - high.astype(F32)).astype(BF16)
    return high, low


def dot(left, right):
    return jnp.dot(left, right, preferred_element_type=F32)


def dot_nt(left, right):
    return lax.dot_general(
        left, right, (((1,), (1,)), ((), ())), preferred_element_type=F32
    )


def left3(value):
    high, low = split(value)
    return jnp.concatenate([high, low, high], axis=1)


def right3(value, axis):
    high, low = split(value)
    return jnp.concatenate([high, high, low], axis=axis)


def right2(value, axis):
    high, low = split(value)
    return jnp.concatenate([high, low], axis=axis)


def kernel(
    n_mesh,
    sub_hbm,
    ritz_hbm,
    ham_hbm,
    connect_hbm,
    rows_hbm,
    out_ref,
    gathered,
    ritz_in,
    ritz_cat,
    ham_in,
    ham_pad,
    connect_in,
    connect_pad,
    rows_in,
    op_sum,
    op_cat,
    op_gg,
    op_og,
    start_acc,
    sends,
    takes,
    local_sem,
    ready,
    own_send,
    own_recv,
    on_send,
    on_recv,
    core_send,
    core_recv,
    halo_send,
    halo_recv,
):
    own_part = lax.axis_index("mesh")
    state = lax.axis_index("state")
    core = lax.rem(state, 2)
    flip = 1 - 2 * core
    sibling = state + flip
    height = lax.div(state, 2)
    across = lax.rem(state + 4, 8)
    above = lax.rem(own_part + 1, n_mesh)
    below = lax.rem(own_part + n_mesh - 1, n_mesh)
    far = lax.rem(own_part + n_mesh // 2, n_mesh)

    def towards(d):
        return lax.rem(state + 2 + 4 * d, 8)

    barrier = pltpu.get_barrier_semaphore()

    def tell(peer):
        pl.semaphore_signal(barrier, inc=1, device_id=peer, device_id_type=MESH)

    def answer(slot, peer):
        pl.semaphore_signal(
            ready.at[slot], inc=1, device_id=peer, device_id_type=MESH
        )

    first_height = height == 0
    last_height = height == 3
    last_part = own_part == n_mesh - 1
    first_part = own_part == 0
    upper_half = own_part >= n_mesh // 2
    tell({"state": sibling})
    pl.when(jnp.logical_not(last_height))(lambda: tell({"state": towards(0)}))
    pl.when(first_height)(lambda: tell({"state": towards(1)}))
    pl.when(jnp.logical_not(last_part))(lambda: tell({"mesh": above}))
    pl.when(first_part)(lambda: tell({"mesh": below}))
    pl.when(jnp.logical_not(upper_half))(lambda: tell({"mesh": far}))

    loads = [
        pltpu.make_async_copy(connect_hbm, connect_in, local_sem.at[0]),
        pltpu.make_async_copy(rows_hbm, rows_in, local_sem.at[1]),
        pltpu.make_async_copy(ham_hbm, ham_in, local_sem.at[2]),
        pltpu.make_async_copy(sub_hbm, gathered.at[state], local_sem.at[3]),
        pltpu.make_async_copy(ritz_hbm, ritz_in, local_sem.at[4]),
    ]
    for load in loads:
        load.start()
    told = (
        1
        + jnp.minimum(height, 1)
        + lax.div(height, 3)
        + jnp.minimum(own_part, 1)
        + lax.div(own_part, n_mesh - 1)
        + lax.div(own_part, n_mesh // 2)
    )
    pl.semaphore_wait(barrier, told)
    pl.when(jnp.logical_not(first_height))(lambda: answer(0, {"state": towards(1)}))
    pl.when(last_height)(lambda: answer(1, {"state": towards(0)}))
    pl.when(jnp.logical_not(first_part))(lambda: answer(2, {"mesh": below}))
    pl.when(last_part)(lambda: answer(3, {"mesh": above}))
    pl.when(upper_half)(lambda: answer(4, {"mesh": far}))

    def answered(slot):
        return lambda: pl.semaphore_wait(ready.at[slot], 1)

    def span(i):
        return pl.ds(pl.multiple_of(i * SIZE, SIZE), SIZE)

    def remote(source, target, send_sem, recv_sem, peer):
        return pltpu.make_async_remote_copy(
            src_ref=source,
            dst_ref=target,
            send_sem=send_sem,
            recv_sem=recv_sem,
            device_id={"state": peer},
            device_id_type=MESH,
        )

    def own_copy(d, i, owner):
        return remote(
            sub_hbm.at[span(i)],
            gathered.at[owner, span(i)],
            own_send.at[d, i],
            own_recv.at[d, i],
            towards(d),
        )

    def on_copy(d, i, owner):
        return remote(
            gathered.at[owner, span(i)],
            gathered.at[owner, span(i)],
            on_send.at[d, i],
            on_recv.at[d, i],
            towards(d),
        )

    def core_copy(kind, i, owner):
        return remote(
            gathered.at[owner, span(i)],
            gathered.at[owner, span(i)],
            core_send.at[kind, i],
            core_recv.at[kind, i],
            sibling,
        )

    own_sibling = remote(
        sub_hbm, gathered.at[state], core_send.at[3, 0], core_recv.at[3, 0], sibling
    )
    started = []

    def start(*copies):
        for copy in copies:
            copy.start()
        started.extend(copies)

    a = jnp.minimum(height, 1)
    b = 1 - a

    def first_half(d):
        return [own_copy(d, SIDE * d + i, state) for i in range(SIDE)]

    def second_half(d):
        return [own_copy(d, SIDE * (1 - d) + i, state) for i in range(SIDE)]

    lead, late = second_half(a), second_half(b)

    def start_lead():
        for copy in lead:
            copy.start()

    pl.when(first_height)(answered(0))
    start(*first_half(a))
    pl.when(first_height)(start_lead)
    start(own_sibling)
    pl.when(first_height)(answered(1))
    pl.when(jnp.logical_and(height > 0, height < 3))(answered(0))
    start(*first_half(b))

    loads[0].wait()
    loads[1].wait()
    connect_pad[...] = jnp.full((16, 128), -1, jnp.int32)
    connect_pad[:, 0:125] = connect_in[...]
    ham_pad[...] = jnp.zeros((16, 128, 128), F32)
    loads[2].wait()
    for e in range(16):
        ham_pad[e, 0:125, 0:125] = ham_in[:, e, :]
    op_sum[...] = jnp.zeros((384, 384), F32)

    def assemble(e, carry):
        names = connect_pad[pl.ds(e, 1), :]
        names = jnp.where(
            names >= 352, names - 32, jnp.where(names >= 320, names + 32, names)
        )
        pick = (
            lax.broadcasted_iota(jnp.int32, (384, 128), 0) == names
        ).astype(F32).astype(BF16)
        high, low = split(ham_pad[e])
        pick2 = jnp.concatenate([pick, pick], axis=1)
        spread = dot_nt(jnp.concatenate([high, low], axis=1), pick2)
        op_sum[...] += dot(pick2, right2(spread, 0))
        return carry

    lax.fori_loop(0, 3, assemble, 0)
    pl.when(jnp.logical_not(first_height))(start_lead)
    started.extend(lead)
    start(*late)
    lax.fori_loop(3, 6, assemble, 0)

    send_names = jnp.concatenate(
        [rows_in[0, pl.ds(k, 1), :] for k in range(4)], axis=1
    )
    place_f = (
        lax.broadcasted_iota(jnp.int32, (256, 128), 0) == send_names
    ).astype(F32)
    place = place_f.astype(BF16)
    take = jnp.transpose(place_f).astype(BF16)
    take2 = jnp.concatenate([take, take], axis=1)
    place2 = jnp.concatenate([place, place], axis=1)
    same = dot(take, place).astype(BF16)
    same2 = jnp.concatenate([same, same], axis=1)
    take_rows2 = jnp.concatenate([take, take], axis=0)

    loads[4].wait()
    for i in range(16):
        ritz_cat[i] = left3(ritz_in[:, 128 * i : 128 * i + 128])

    def rotate(owner, h):
        rows = gathered[owner, pl.ds(pl.multiple_of(128 * h, 128), 128), :]
        start_acc[...] += dot(ritz_cat[2 * owner + h], right3(rows, 0))

    start_acc[...] = jnp.zeros((128, 256), F32)
    loads[3].wait()
    rotate(state, 0)
    rotate(state, 1)

    from_a, from_b = towards(a), towards(b)
    for i in range(SIDE):
        for d, owner in ((b, from_a), (a, from_b)):
            k = SIDE * d + i
            own_copy(d, k, owner).wait_recv()
            start(on_copy(d, k, owner), core_copy(d, k, owner))
        lax.fori_loop(6 + 2 * i, 8 + 2 * i, assemble, 0)
    own_sibling.wait_recv()
    rotate(sibling, 0)
    rotate(sibling, 1)
    rotate(from_a, b)
    rotate(from_b, a)
    lax.fori_loop(6 + 2 * SIDE, 16, assemble, 0)
    for i in range(SIDE):
        for d, owner in ((b, from_a), (a, from_b)):
            k = SIDE * (1 - d) + i
            own_copy(d, k, owner).wait_recv()
            start(core_copy(d, k, owner))
    rotate(from_a, a)
    rotate(from_b, b)
    for d, owner in ((b, from_a), (a, from_b)):
        for i in range(SIDE):
            core_copy(d, SIDE * d + i, owner + flip).wait_recv()
        rotate(owner + flip, d)
    centre = 2.5
    eye = (
        lax.broadcasted_iota(jnp.int32, (384, 256), 0)
        == lax.broadcasted_iota(jnp.int32, (384, 256), 1)
    ).astype(F32)
    op_cat[...] = left3(op_sum[:, 0:256] - centre * eye)
    ghost_cols = left3(op_sum[:, 256:384])
    op_og[...] = ghost_cols[0:256]
    op_gg[...] = ghost_cols[256:384]

    for d, owner in ((b, from_a), (a, from_b)):
        for i in range(SIDE):
            core_copy(d, SIDE * (1 - d) + i, owner + flip).wait_recv()
        rotate(owner + flip, 1 - d)
    for i in range(SIDE):
        for d in (b, a):
            k = SIDE * d + i
            on_copy(d, k, across).wait_recv()
            start(core_copy(2, k, across))
    pl.when(jnp.logical_not(last_part))(answered(2))
    pl.when(first_part)(answered(3))
    pl.when(jnp.logical_not(upper_half))(answered(4))
    rotate(across, 0)
    rotate(across, 1)
    for h in range(2):
        for i in range(SIDE):
            core_copy(2, SIDE * h + i, across + flip).wait_recv()
        rotate(across + flip, h)

    block = start_acc[...]

    def exchange(number):
        copies = []
        for k, (first, count, target, peer) in enumerate(
            ((0, 32, 32, above), (32, 32, 0, below), (64, 64, 64, far))
        ):
            copies.append(
                pltpu.make_async_remote_copy(
                    src_ref=sends.at[number, pl.ds(first, count)],
                    dst_ref=takes.at[number, pl.ds(target, count)],
                    send_sem=halo_send.at[number, k],
                    recv_sem=halo_recv.at[number, k],
                    device_id={"mesh": peer},
                    device_id_type=MESH,
                )
            )
        start(*copies)
        return copies

    def arrive(copies):
        for copy in copies:
            copy.wait_recv()
        return takes[len(halos) - 1]

    sigma_one = 1.5 / (-1.0 - centre)
    sigma_two = 1.0 / (2.0 / sigma_one - sigma_one)
    scale_one = sigma_one / 1.5
    scale_two = 2.0 * sigma_two / 1.5
    halos = []

    sends[0] = dot_nt(take2, right2(block, 1))
    halos.append(exchange(0))
    base = dot_nt(op_cat[...], right3(block, 1))
    ghosts = right3(arrive(halos[0]), 0)
    sends[1] = base[256:384] + dot(op_gg[...], ghosts)
    halos.append(exchange(1))
    own = base[0:256] + dot(op_og[...], ghosts)
    own_packed = dot(take2, right2(own, 0))
    back = right2(arrive(halos[1]), 0)
    sends[2] = scale_one * (own_packed + dot(same2, back))
    halos.append(exchange(2))
    first = scale_one * (own + dot(place2, back))
    base = dot(op_cat[...], right3(first, 0))
    ghosts = right3(arrive(halos[2]), 0)
    sends[3] = base[256:384] + dot(op_gg[...], ghosts)
    halos.append(exchange(3))
    own = base[0:256] + dot(op_og[...], ghosts)
    rest = scale_two * jnp.transpose(own) - sigma_one * sigma_two * block
    back = right2(jnp.transpose(arrive(halos[3])), 1)
    out_ref[...] = rest + scale_two * dot(back, take_rows2)

    for copy in started:
        copy.wait_send()


def solution(mesh):
    n_mesh = mesh.shape["mesh"]

    def per_device(subspace, ritz, element_ham, connect, send_rows):
        any_space = pl.BlockSpec(memory_space=pl.ANY)
        hams = jnp.transpose(element_ham, (1, 0, 2))
        return pl.pallas_call(
            functools.partial(kernel, n_mesh),
            out_shape=jax.ShapeDtypeStruct((128, 256), F32),
            in_specs=[any_space] * 5,
            out_specs=pl.BlockSpec(memory_space=pltpu.VMEM),
            scratch_shapes=[
                pltpu.VMEM((8, 256, 256), F32),
                pltpu.VMEM((128, 2048), F32),
                pltpu.VMEM((16, 128, 384), BF16),
                pltpu.VMEM((125, 16, 125), F32),
                pltpu.VMEM((16, 128, 128), F32),
                pltpu.VMEM((16, 125), jnp.int32),
                pltpu.VMEM((16, 128), jnp.int32),
                pltpu.VMEM((1, 4, 32), jnp.int32),
                pltpu.VMEM((384, 384), F32),
                pltpu.VMEM((384, 768), BF16),
                pltpu.VMEM((128, 384), BF16),
                pltpu.VMEM((256, 384), BF16),
                pltpu.VMEM((128, 256), F32),
                pltpu.VMEM((4, 128, 128), F32),
                pltpu.VMEM((4, 128, 128), F32),
                pltpu.SemaphoreType.DMA((5,)),
                pltpu.SemaphoreType.REGULAR((5,)),
                pltpu.SemaphoreType.DMA((2, PIECES)),
                pltpu.SemaphoreType.DMA((2, PIECES)),
                pltpu.SemaphoreType.DMA((2, PIECES)),
                pltpu.SemaphoreType.DMA((2, PIECES)),
                pltpu.SemaphoreType.DMA((4, PIECES)),
                pltpu.SemaphoreType.DMA((4, PIECES)),
                pltpu.SemaphoreType.DMA((4, 3)),
                pltpu.SemaphoreType.DMA((4, 3)),
            ],
            compiler_params=pltpu.CompilerParams(
                collective_id=0,
                has_side_effects=True,
                vmem_limit_bytes=60 * 1024 * 1024,
            ),
        )(subspace, ritz, hams, connect, send_rows)

    return jax.shard_map(
        per_device,
        mesh=mesh,
        in_specs=(
            P("state", "mesh"),
            P("state", None),
            P("mesh", None, None),
            P("mesh", None),
            P("mesh", None, None),
        ),
        out_specs=P("state", "mesh"),
        check_vma=False,
    )
```

```python
import functools

import jax
import jax.numpy as jnp
from jax import lax
from jax.experimental import pallas as pl
from jax.experimental.pallas import tpu as pltpu
from jax.sharding import PartitionSpec as P

MESH = pl.DeviceIdType.MESH
F32 = jnp.float32
BF16 = jnp.bfloat16
PIECES = 4
SIDE = PIECES // 2
SIZE = 256 // PIECES


def split(value):
    high = value.astype(BF16)
    low = (value - high.astype(F32)).astype(BF16)
    return high, low


def dot(left, right):
    return jnp.dot(left, right, preferred_element_type=F32)


def dot_nt(left, right):
    return lax.dot_general(
        left, right, (((1,), (1,)), ((), ())), preferred_element_type=F32
    )


def left3(value):
    high, low = split(value)
    return jnp.concatenate([high, low, high], axis=1)


def right3(value, axis):
    high, low = split(value)
    return jnp.concatenate([high, high, low], axis=axis)


def right2(value, axis):
    high, low = split(value)
    return jnp.concatenate([high, low], axis=axis)


def kernel(
    n_mesh,
    sub_hbm,
    ritz_hbm,
    ham_hbm,
    connect_hbm,
    rows_hbm,
    out_ref,
    gathered,
    ritz_in,
    ritz_cat,
    ham_in,
    ham_pad,
    connect_in,
    connect_pad,
    rows_in,
    op_sum,
    op_cat,
    op_gg,
    op_og,
    start_acc,
    sends,
    takes,
    local_sem,
    ready,
    own_send,
    own_recv,
    on_send,
    on_recv,
    core_send,
    core_recv,
    halo_send,
    halo_recv,
):
    own_part = lax.axis_index("mesh")
    state = lax.axis_index("state")
    core = lax.rem(state, 2)
    flip = 1 - 2 * core
    sibling = state + flip
    height = lax.div(state, 2)
    across = lax.rem(state + 4, 8)
    above = lax.rem(own_part + 1, n_mesh)
    below = lax.rem(own_part + n_mesh - 1, n_mesh)
    far = lax.rem(own_part + n_mesh // 2, n_mesh)

    def towards(d):
        return lax.rem(state + 2 + 4 * d, 8)

    barrier = pltpu.get_barrier_semaphore()

    def tell(peer):
        pl.semaphore_signal(barrier, inc=1, device_id=peer, device_id_type=MESH)

    def answer(slot, peer):
        pl.semaphore_signal(
            ready.at[slot], inc=1, device_id=peer, device_id_type=MESH
        )

    first_height = height == 0
    last_height = height == 3
    last_part = own_part == n_mesh - 1
    first_part = own_part == 0
    upper_half = own_part >= n_mesh // 2
    tell({"state": sibling})
    pl.when(jnp.logical_not(last_height))(lambda: tell({"state": towards(0)}))
    pl.when(first_height)(lambda: tell({"state": towards(1)}))
    pl.when(jnp.logical_not(last_part))(lambda: tell({"mesh": above}))
    pl.when(first_part)(lambda: tell({"mesh": below}))
    pl.when(jnp.logical_not(upper_half))(lambda: tell({"mesh": far}))

    loads = [
        pltpu.make_async_copy(connect_hbm, connect_in, local_sem.at[0]),
        pltpu.make_async_copy(rows_hbm, rows_in, local_sem.at[1]),
        pltpu.make_async_copy(ham_hbm, ham_in, local_sem.at[2]),
        pltpu.make_async_copy(sub_hbm, gathered.at[state], local_sem.at[3]),
        pltpu.make_async_copy(ritz_hbm, ritz_in, local_sem.at[4]),
    ]
    for load in loads:
        load.start()
    told = (
        1
        + jnp.minimum(height, 1)
        + lax.div(height, 3)
        + jnp.minimum(own_part, 1)
        + lax.div(own_part, n_mesh - 1)
        + lax.div(own_part, n_mesh // 2)
    )
    pl.semaphore_wait(barrier, told)
    pl.when(jnp.logical_not(first_height))(lambda: answer(0, {"state": towards(1)}))
    pl.when(last_height)(lambda: answer(1, {"state": towards(0)}))
    pl.when(jnp.logical_not(first_part))(lambda: answer(2, {"mesh": below}))
    pl.when(last_part)(lambda: answer(3, {"mesh": above}))
    pl.when(upper_half)(lambda: answer(4, {"mesh": far}))

    def answered(slot):
        return lambda: pl.semaphore_wait(ready.at[slot], 1)

    def span(i):
        return pl.ds(pl.multiple_of(i * SIZE, SIZE), SIZE)

    def remote(source, target, send_sem, recv_sem, peer):
        return pltpu.make_async_remote_copy(
            src_ref=source,
            dst_ref=target,
            send_sem=send_sem,
            recv_sem=recv_sem,
            device_id={"state": peer},
            device_id_type=MESH,
        )

    def own_copy(d, i, owner):
        return remote(
            sub_hbm.at[span(i)],
            gathered.at[owner, span(i)],
            own_send.at[d, i],
            own_recv.at[d, i],
            towards(d),
        )

    def on_copy(d, i, owner):
        return remote(
            gathered.at[owner, span(i)],
            gathered.at[owner, span(i)],
            on_send.at[d, i],
            on_recv.at[d, i],
            towards(d),
        )

    def core_copy(kind, i, owner):
        return remote(
            gathered.at[owner, span(i)],
            gathered.at[owner, span(i)],
            core_send.at[kind, i],
            core_recv.at[kind, i],
            sibling,
        )

    own_sibling = remote(
        sub_hbm, gathered.at[state], core_send.at[3, 0], core_recv.at[3, 0], sibling
    )
    started = []

    def start(*copies):
        for copy in copies:
            copy.start()
        started.extend(copies)

    a = jnp.minimum(height, 1)
    b = 1 - a

    def first_half(d):
        return [own_copy(d, SIDE * d + i, state) for i in range(SIDE)]

    def second_half(d):
        return [own_copy(d, SIDE * (1 - d) + i, state) for i in range(SIDE)]

    lead, late = second_half(a), second_half(b)

    def start_lead():
        for copy in lead:
            copy.start()

    pl.when(first_height)(answered(0))
    start(*first_half(a))
    pl.when(first_height)(start_lead)
    start(own_sibling)
    pl.when(first_height)(answered(1))
    pl.when(jnp.logical_and(height > 0, height < 3))(answered(0))
    start(*first_half(b))

    loads[0].wait()
    loads[1].wait()
    connect_pad[...] = jnp.full((16, 128), -1, jnp.int32)
    connect_pad[:, 0:125] = connect_in[...]
    ham_pad[...] = jnp.zeros((16, 128, 128), F32)
    loads[2].wait()
    for e in range(16):
        ham_pad[e, 0:125, 0:125] = ham_in[:, e, :]
    op_sum[...] = jnp.zeros((384, 384), F32)

    def assemble(e, carry):
        names = connect_pad[pl.ds(e, 1), :]
        names = jnp.where(
            names >= 352, names - 32, jnp.where(names >= 320, names + 32, names)
        )
        pick = (
            lax.broadcasted_iota(jnp.int32, (384, 128), 0) == names
        ).astype(F32).astype(BF16)
        high, low = split(ham_pad[e])
        pick2 = jnp.concatenate([pick, pick], axis=1)
        spread = dot_nt(jnp.concatenate([high, low], axis=1), pick2)
        op_sum[...] += dot(pick2, right2(spread, 0))
        return carry

    lax.fori_loop(0, 3, assemble, 0)
    pl.when(jnp.logical_not(first_height))(start_lead)
    started.extend(lead)
    start(*late)
    lax.fori_loop(3, 6, assemble, 0)

    send_names = jnp.concatenate(
        [rows_in[0, pl.ds(k, 1), :] for k in range(4)], axis=1
    )
    place_f = (
        lax.broadcasted_iota(jnp.int32, (256, 128), 0) == send_names
    ).astype(F32)
    place = place_f.astype(BF16)
    take = jnp.transpose(place_f).astype(BF16)
    take2 = jnp.concatenate([take, take], axis=1)
    place2 = jnp.concatenate([place, place], axis=1)
    same = dot(take, place).astype(BF16)
    same2 = jnp.concatenate([same, same], axis=1)
    take_rows2 = jnp.concatenate([take, take], axis=0)

    loads[4].wait()
    for i in range(16):
        ritz_cat[i] = left3(ritz_in[:, 128 * i : 128 * i + 128])

    def rotate(owner, h):
        rows = gathered[owner, pl.ds(pl.multiple_of(128 * h, 128), 128), :]
        start_acc[...] += dot(ritz_cat[2 * owner + h], right3(rows, 0))

    start_acc[...] = jnp.zeros((128, 256), F32)
    loads[3].wait()
    rotate(state, 0)
    rotate(state, 1)

    from_a, from_b = towards(a), towards(b)
    for i in range(SIDE):
        for d, owner in ((b, from_a), (a, from_b)):
            k = SIDE * d + i
            own_copy(d, k, owner).wait_recv()
            start(on_copy(d, k, owner), core_copy(d, k, owner))
        lax.fori_loop(6 + 8 * i // SIDE, 6 + 8 * (i + 1) // SIDE, assemble, 0)
    own_sibling.wait_recv()
    rotate(sibling, 0)
    rotate(sibling, 1)
    rotate(from_a, b)
    rotate(from_b, a)
    lax.fori_loop(14, 16, assemble, 0)
    for i in range(SIDE):
        for d, owner in ((b, from_a), (a, from_b)):
            k = SIDE * (1 - d) + i
            own_copy(d, k, owner).wait_recv()
            start(core_copy(d, k, owner))
    rotate(from_a, a)
    rotate(from_b, b)
    for d, owner in ((b, from_a), (a, from_b)):
        for i in range(SIDE):
            core_copy(d, SIDE * d + i, owner + flip).wait_recv()
        rotate(owner + flip, d)
    centre = 2.5
    eye = (
        lax.broadcasted_iota(jnp.int32, (384, 256), 0)
        == lax.broadcasted_iota(jnp.int32, (384, 256), 1)
    ).astype(F32)
    op_cat[...] = left3(op_sum[:, 0:256] - centre * eye)
    ghost_cols = left3(op_sum[:, 256:384])
    op_og[...] = ghost_cols[0:256]
    op_gg[...] = ghost_cols[256:384]

    for d, owner in ((b, from_a), (a, from_b)):
        for i in range(SIDE):
            core_copy(d, SIDE * (1 - d) + i, owner + flip).wait_recv()
        rotate(owner + flip, 1 - d)
    for i in range(SIDE):
        for d in (b, a):
            k = SIDE * d + i
            on_copy(d, k, across).wait_recv()
            start(core_copy(2, k, across))
    pl.when(jnp.logical_not(last_part))(answered(2))
    pl.when(first_part)(answered(3))
    pl.when(jnp.logical_not(upper_half))(answered(4))
    rotate(across, 0)
    rotate(across, 1)
    for h in range(2):
        for i in range(SIDE):
            core_copy(2, SIDE * h + i, across + flip).wait_recv()
        rotate(across + flip, h)

    block = start_acc[...]

    def exchange(number):
        copies = []
        for k, (first, count, target, peer) in enumerate(
            ((64, 64, 64, far), (0, 32, 32, above), (32, 32, 0, below))
        ):
            copies.append(
                pltpu.make_async_remote_copy(
                    src_ref=sends.at[number, pl.ds(first, count)],
                    dst_ref=takes.at[number, pl.ds(target, count)],
                    send_sem=halo_send.at[number, k],
                    recv_sem=halo_recv.at[number, k],
                    device_id={"mesh": peer},
                    device_id_type=MESH,
                )
            )
        start(*copies)
        return copies

    def arrive(copies):
        for copy in copies:
            copy.wait_recv()
        return takes[len(halos) - 1]

    sigma_one = 1.5 / (-1.0 - centre)
    sigma_two = 1.0 / (2.0 / sigma_one - sigma_one)
    scale_one = sigma_one / 1.5
    scale_two = 2.0 * sigma_two / 1.5
    halos = []

    sends[0] = dot_nt(take2, right2(block, 1))
    halos.append(exchange(0))
    base = dot_nt(op_cat[...], right3(block, 1))
    ghosts = right3(arrive(halos[0]), 0)
    sends[1] = base[256:384] + dot(op_gg[...], ghosts)
    halos.append(exchange(1))
    own = base[0:256] + dot(op_og[...], ghosts)
    own_packed = dot(take2, right2(own, 0))
    back = right2(arrive(halos[1]), 0)
    sends[2] = scale_one * (own_packed + dot(same2, back))
    halos.append(exchange(2))
    first = scale_one * (own + dot(place2, back))
    base = dot(op_cat[...], right3(first, 0))
    ghosts = right3(arrive(halos[2]), 0)
    sends[3] = base[256:384] + dot(op_gg[...], ghosts)
    halos.append(exchange(3))
    own = base[0:256] + dot(op_og[...], ghosts)
    rest = scale_two * jnp.transpose(own) - sigma_one * sigma_two * block
    back = right2(jnp.transpose(arrive(halos[3])), 1)
    out_ref[...] = rest + scale_two * dot(back, take_rows2)

    for copy in started:
        copy.wait_send()


def solution(mesh):
    n_mesh = mesh.shape["mesh"]

    def per_device(subspace, ritz, element_ham, connect, send_rows):
        any_space = pl.BlockSpec(memory_space=pl.ANY)
        hams = jnp.transpose(element_ham, (1, 0, 2))
        return pl.pallas_call(
            functools.partial(kernel, n_mesh),
            out_shape=pltpu.VMEM((128, 256), F32),
            in_specs=[any_space] * 5,
            out_specs=pl.BlockSpec(memory_space=pltpu.VMEM),
            scratch_shapes=[
                pltpu.VMEM((8, 256, 256), F32),
                pltpu.VMEM((128, 2048), F32),
                pltpu.VMEM((16, 128, 384), BF16),
                pltpu.VMEM((125, 16, 125), F32),
                pltpu.VMEM((16, 128, 128), F32),
                pltpu.VMEM((16, 125), jnp.int32),
                pltpu.VMEM((16, 128), jnp.int32),
                pltpu.VMEM((1, 4, 32), jnp.int32),
                pltpu.VMEM((384, 384), F32),
                pltpu.VMEM((384, 768), BF16),
                pltpu.VMEM((128, 384), BF16),
                pltpu.VMEM((256, 384), BF16),
                pltpu.VMEM((128, 256), F32),
                pltpu.VMEM((4, 128, 128), F32),
                pltpu.VMEM((4, 128, 128), F32),
                pltpu.SemaphoreType.DMA((5,)),
                pltpu.SemaphoreType.REGULAR((5,)),
                pltpu.SemaphoreType.DMA((2, PIECES)),
                pltpu.SemaphoreType.DMA((2, PIECES)),
                pltpu.SemaphoreType.DMA((2, PIECES)),
                pltpu.SemaphoreType.DMA((2, PIECES)),
                pltpu.SemaphoreType.DMA((4, PIECES)),
                pltpu.SemaphoreType.DMA((4, PIECES)),
                pltpu.SemaphoreType.DMA((4, 3)),
                pltpu.SemaphoreType.DMA((4, 3)),
            ],
            compiler_params=pltpu.CompilerParams(
                collective_id=0,
                has_side_effects=True,
                vmem_limit_bytes=60 * 1024 * 1024,
            ),
        )(subspace, ritz, hams, connect, send_rows)

    return jax.shard_map(
        per_device,
        mesh=mesh,
        in_specs=(
            P("state", "mesh"),
            P("state", None),
            P("mesh", None, None),
            P("mesh", None),
            P("mesh", None, None),
        ),
        out_specs=P("state", "mesh"),
        check_vma=False,
    )
```

```python
import functools

import jax
import jax.numpy as jnp
from jax import lax
from jax.experimental import pallas as pl
from jax.experimental.pallas import tpu as pltpu
from jax.sharding import PartitionSpec as P

MESH = pl.DeviceIdType.MESH
F32 = jnp.float32
BF16 = jnp.bfloat16
SIZE = 64
GROUP = 4


def split(value):
    high = value.astype(BF16)
    low = (value - high.astype(F32)).astype(BF16)
    return high, low


def dot(left, right):
    return jnp.dot(left, right, preferred_element_type=F32)


def dot_nt(left, right):
    return lax.dot_general(
        left, right, (((1,), (1,)), ((), ())), preferred_element_type=F32
    )


def left3(value):
    high, low = split(value)
    return jnp.concatenate([high, low, high], axis=1)


def right3(value, axis):
    high, low = split(value)
    return jnp.concatenate([high, high, low], axis=axis)


def right2(value, axis):
    high, low = split(value)
    return jnp.concatenate([high, low], axis=axis)


def kernel(
    n_mesh,
    sub_hbm,
    ritz_hbm,
    ham_hbm,
    connect_hbm,
    rows_hbm,
    out_ref,
    gathered,
    ritz_in,
    ritz_cat,
    ham_in,
    ham_pad,
    connect_in,
    connect_pad,
    rows_in,
    op_sum,
    op_cat,
    op_gg,
    op_og,
    same2,
    raw_part,
    start_acc,
    out_acc,
    sends,
    takes,
    local_sem,
    ready,
    own_send,
    own_recv,
    on_send,
    on_recv,
    core_send,
    core_recv,
    halo_send,
    halo_recv,
):
    own_part = lax.axis_index("mesh")
    state = lax.axis_index("state")
    core = lax.rem(state, 2)
    flip = 1 - 2 * core
    sibling = state + flip
    height = lax.div(state, 2)
    across = lax.rem(state + 4, 8)
    above = lax.rem(own_part + 1, n_mesh)
    below = lax.rem(own_part + n_mesh - 1, n_mesh)
    far = lax.rem(own_part + n_mesh // 2, n_mesh)

    def towards(d):
        return lax.rem(state + 2 + 4 * d, 8)

    barrier = pltpu.get_barrier_semaphore()

    def tell(peer):
        pl.semaphore_signal(barrier, inc=1, device_id=peer, device_id_type=MESH)

    def answer(slot, peer):
        pl.semaphore_signal(
            ready.at[slot], inc=1, device_id=peer, device_id_type=MESH
        )

    first_height = height == 0
    last_height = height == 3
    last_part = own_part == n_mesh - 1
    first_part = own_part == 0
    upper_half = own_part >= n_mesh // 2
    tell({"state": sibling})
    pl.when(jnp.logical_not(last_height))(lambda: tell({"state": towards(0)}))
    pl.when(first_height)(lambda: tell({"state": towards(1)}))
    pl.when(jnp.logical_not(last_part))(lambda: tell({"mesh": above}))
    pl.when(first_part)(lambda: tell({"mesh": below}))
    pl.when(jnp.logical_not(upper_half))(lambda: tell({"mesh": far}))

    loads = [
        pltpu.make_async_copy(rows_hbm, rows_in, local_sem.at[0]),
        pltpu.make_async_copy(sub_hbm.at[pl.ds(128, 128)], raw_part, local_sem.at[1]),
        pltpu.make_async_copy(connect_hbm, connect_in, local_sem.at[2]),
        pltpu.make_async_copy(ham_hbm, ham_in, local_sem.at[3]),
        pltpu.make_async_copy(
            sub_hbm.at[pl.ds(0, 128)], gathered.at[state, pl.ds(0, 128)], local_sem.at[4]
        ),
        pltpu.make_async_copy(ritz_hbm, ritz_in, local_sem.at[5]),
    ]
    for load in loads:
        load.start()
    told = (
        1
        + jnp.minimum(height, 1)
        + lax.div(height, 3)
        + jnp.minimum(own_part, 1)
        + lax.div(own_part, n_mesh - 1)
        + lax.div(own_part, n_mesh // 2)
    )
    pl.semaphore_wait(barrier, told)
    pl.when(jnp.logical_not(first_height))(lambda: answer(0, {"state": towards(1)}))
    pl.when(last_height)(lambda: answer(1, {"state": towards(0)}))
    pl.when(jnp.logical_not(first_part))(lambda: answer(2, {"mesh": below}))
    pl.when(last_part)(lambda: answer(3, {"mesh": above}))
    pl.when(upper_half)(lambda: answer(4, {"mesh": far}))

    def answered(slot):
        return lambda: pl.semaphore_wait(ready.at[slot], 1)

    def span(part, i):
        return pl.ds(pl.multiple_of(128 * part + SIZE * i, SIZE), SIZE)

    def remote(source, target, send_sem, recv_sem, peer):
        return pltpu.make_async_remote_copy(
            src_ref=source,
            dst_ref=target,
            send_sem=send_sem,
            recv_sem=recv_sem,
            device_id={"state": peer},
            device_id_type=MESH,
        )

    def own_copy(part, d, i, owner):
        target = gathered.at[owner, span(part, i)]
        return remote(
            target if part else sub_hbm.at[span(part, i)],
            target,
            own_send.at[part, d, i],
            own_recv.at[part, d, i],
            towards(d),
        )

    def on_copy(part, d, owner):
        target = gathered.at[owner, span(part, d)]
        return remote(
            target, target, on_send.at[part, d], on_recv.at[part, d], towards(d)
        )

    def core_copy(part, kind, i, owner):
        target = gathered.at[owner, span(part, i)]
        return remote(
            target,
            target,
            core_send.at[part, kind, i],
            core_recv.at[part, kind, i],
            sibling,
        )

    def own_sibling(part, owner):
        rows = pl.ds(128 * part, 128)
        target = gathered.at[owner, rows]
        return remote(
            target if part else sub_hbm.at[rows],
            target,
            core_send.at[part, 3, 0],
            core_recv.at[part, 3, 0],
            sibling,
        )

    started = []

    def start(*copies):
        for copy in copies:
            copy.start()
        started.extend(copies)

    a = jnp.minimum(height, 1)
    b = 1 - a
    from_a, from_b = towards(a), towards(b)
    higher = jnp.logical_not(first_height)

    late_first = own_copy(0, b, b, state)
    late_second = own_copy(0, b, a, state)
    pl.when(first_height)(answered(0))
    start(own_copy(0, a, a, state), own_sibling(0, state))
    pl.when(jnp.logical_and(height > 0, height < 3))(answered(0))
    pl.when(higher)(late_first.start)

    def service_first(part):
        for d, owner in ((b, from_a), (a, from_b)):
            own_copy(part, d, d, owner).wait_recv()
            start(on_copy(part, d, owner), core_copy(part, d, d, owner))

    def service_second(part):
        for d, owner in ((b, from_a), (a, from_b)):
            own_copy(part, d, 1 - d, owner).wait_recv()
            start(core_copy(part, d, 1 - d, owner))

    def service_far(part):
        for d in (b, a):
            on_copy(part, d, across).wait_recv()
            start(core_copy(part, 2, d, across))

    def rotate(total, part, owner):
        rows = gathered[owner, 128 * part : 128 * part + 128, :]
        total[...] += dot(ritz_cat[2 * owner + part], right3(rows, 0))

    def rotate_sibling(total, part):
        own_sibling(part, sibling).wait_recv()
        rotate(total, part, sibling)

    def rotate_near(total, part):
        rotate(total, part, from_a)
        rotate(total, part, from_b)

    def rotate_rest(total, part):
        for d, owner in ((b, from_a), (a, from_b)):
            for i in range(2):
                core_copy(part, d, i, owner + flip).wait_recv()
            rotate(total, part, owner + flip)
        rotate(total, part, across)
        for i in range(2):
            core_copy(part, 2, i, across + flip).wait_recv()
        rotate(total, part, across + flip)

    loads[0].wait()
    send_names = jnp.concatenate(
        [rows_in[0, pl.ds(k, 1), :] for k in range(4)], axis=1
    )
    place_f = (
        lax.broadcasted_iota(jnp.int32, (256, 128), 0) == send_names
    ).astype(F32)
    place = place_f.astype(BF16)
    take = jnp.transpose(place_f).astype(BF16)
    take2 = jnp.concatenate([take, take], axis=1)
    place2 = jnp.concatenate([place, place], axis=1)
    take_rows2 = jnp.concatenate([take, take], axis=0)

    def exchange(number):
        copies = []
        for k, (first, count, target, peer) in enumerate(
            ((64, 64, 64, far), (0, 32, 32, above), (32, 32, 0, below))
        ):
            copies.append(
                pltpu.make_async_remote_copy(
                    src_ref=sends.at[number, pl.ds(first, count)],
                    dst_ref=takes.at[number, pl.ds(target, count)],
                    send_sem=halo_send.at[number, k],
                    recv_sem=halo_recv.at[number, k],
                    device_id={"mesh": peer},
                    device_id_type=MESH,
                )
            )
        start(*copies)
        return copies

    centre = 2.5
    sigma_one = 1.5 / (-1.0 - centre)
    sigma_two = 1.0 / (2.0 / sigma_one - sigma_one)
    scale_one = sigma_one / 1.5
    scale_two = 2.0 * sigma_two / 1.5

    class Chain:
        def __init__(self, values, number):
            self.values, self.number, self.copies = values, number, None

        def send(self, value):
            sends[self.number] = value
            self.copies = exchange(self.number)
            self.number += 1

        def arrived(self):
            for copy in self.copies:
                copy.wait_recv()
            return takes[self.number - 1]

        def fetch(self):
            self.send(dot_nt(take2, right2(self.values[...], 1)))

        def apply_first(self):
            self.base = dot_nt(op_cat[...], right3(self.values[...], 1))

        def give_first(self):
            ghosts = right3(self.arrived(), 0)
            self.send(self.base[256:384] + dot(op_gg[...], ghosts))
            self.own = self.base[0:256] + dot(op_og[...], ghosts)
            self.packed = dot(take2, right2(self.own, 0))

        def fetch_second(self):
            back = right2(self.arrived(), 0)
            self.send(scale_one * (self.packed + dot(same2[...], back)))
            first = scale_one * (self.own + dot(place2, back))
            self.base = dot(op_cat[...], right3(first, 0))

        def give_second(self):
            ghosts = right3(self.arrived(), 0)
            self.send(self.base[256:384] + dot(op_gg[...], ghosts))
            own = self.base[0:256] + dot(op_og[...], ghosts)
            self.rest = (
                scale_two * jnp.transpose(own)
                - sigma_one * sigma_two * self.values[...]
            )

        def finish(self):
            back = right2(jnp.transpose(self.arrived()), 1)
            return self.rest + scale_two * dot(back, take_rows2)

    chain = Chain(raw_part, 0)
    loads[1].wait()
    pl.when(jnp.logical_not(last_part))(answered(2))
    pl.when(first_part)(answered(3))
    pl.when(jnp.logical_not(upper_half))(answered(4))
    chain.fetch()
    start(own_copy(0, a, b, state))
    pl.when(higher)(late_second.start)
    started.extend([late_first, late_second])
    same = dot(take, place).astype(BF16)
    same2[...] = jnp.concatenate([same, same], axis=1)

    loads[2].wait()
    connect_pad[...] = jnp.full((16, 128), -1, jnp.int32)
    connect_pad[:, 0:125] = connect_in[...]
    ham_pad[...] = jnp.zeros((16, 128, 128), F32)
    loads[3].wait()
    for e in range(16):
        ham_pad[e, 0:125, 0:125] = ham_in[:, e, :]
    op_sum[...] = jnp.zeros((384, 384), F32)

    def assemble(g, carry):
        picks, spreads = [], []
        for q in range(GROUP):
            e = GROUP * g + q
            names = connect_pad[pl.ds(e, 1), :]
            names = jnp.where(
                names >= 352, names - 32, jnp.where(names >= 320, names + 32, names)
            )
            pick = (
                lax.broadcasted_iota(jnp.int32, (384, 128), 0) == names
            ).astype(F32).astype(BF16)
            high, low = split(ham_pad[e])
            pick2 = jnp.concatenate([pick, pick], axis=1)
            spread = dot_nt(jnp.concatenate([high, low], axis=1), pick2)
            picks.append(pick2)
            spreads.append(right2(spread, 0))
        op_sum[...] += dot(
            jnp.concatenate(picks, axis=1), jnp.concatenate(spreads, axis=0)
        )
        return carry

    lax.fori_loop(0, 16 // GROUP, assemble, 0)

    def start_late():
        pl.semaphore_wait(ready.at[1], 1)
        late_first.start()
        late_second.start()

    pl.when(first_height)(start_late)

    eye = (
        lax.broadcasted_iota(jnp.int32, (384, 256), 0)
        == lax.broadcasted_iota(jnp.int32, (384, 256), 1)
    ).astype(F32)
    op_cat[...] = left3(op_sum[:, 0:256] - centre * eye)
    ghost_cols = left3(op_sum[:, 256:384])
    op_og[...] = ghost_cols[0:256]
    op_gg[...] = ghost_cols[256:384]

    chain.apply_first()
    chain.give_first()
    service_first(0)
    loads[5].wait()
    for i in range(16):
        ritz_cat[i] = left3(ritz_in[:, 128 * i : 128 * i + 128])
    start_acc[...] = jnp.zeros((128, 256), F32)
    out_acc[...] = jnp.zeros((128, 256), F32)
    loads[4].wait()
    rotate(start_acc, 0, state)
    rotate_sibling(start_acc, 0)
    chain.fetch_second()
    service_second(0)
    rotate_near(start_acc, 0)
    chain.give_second()
    service_far(0)
    rotate_rest(start_acc, 0)

    main = Chain(start_acc, 4)
    main.fetch()
    gathered[state, 128:256, :] = chain.finish()
    start(
        own_copy(1, b, b, state),
        own_copy(1, a, a, state),
        own_sibling(1, state),
        own_copy(1, b, a, state),
        own_copy(1, a, b, state),
    )
    main.apply_first()
    main.give_first()
    rotate(out_acc, 1, state)
    main.fetch_second()
    service_first(1)
    rotate_sibling(out_acc, 1)
    main.give_second()
    service_second(1)
    rotate_near(out_acc, 1)
    service_far(1)
    rotate_rest(out_acc, 1)
    out_ref[...] = main.finish() + out_acc[...]

    for copy in started:
        copy.wait_send()


def solution(mesh):
    n_mesh = mesh.shape["mesh"]

    def per_device(subspace, ritz, element_ham, connect, send_rows):
        any_space = pl.BlockSpec(memory_space=pl.ANY)
        hams = jnp.transpose(element_ham, (1, 0, 2))
        return pl.pallas_call(
            functools.partial(kernel, n_mesh),
            out_shape=pltpu.VMEM((128, 256), F32),
            in_specs=[any_space] * 5,
            out_specs=pl.BlockSpec(memory_space=pltpu.VMEM),
            scratch_shapes=[
                pltpu.VMEM((8, 256, 256), F32),
                pltpu.VMEM((128, 2048), F32),
                pltpu.VMEM((16, 128, 384), BF16),
                pltpu.VMEM((125, 16, 125), F32),
                pltpu.VMEM((16, 128, 128), F32),
                pltpu.VMEM((16, 125), jnp.int32),
                pltpu.VMEM((16, 128), jnp.int32),
                pltpu.VMEM((1, 4, 32), jnp.int32),
                pltpu.VMEM((384, 384), F32),
                pltpu.VMEM((384, 768), BF16),
                pltpu.VMEM((128, 384), BF16),
                pltpu.VMEM((256, 384), BF16),
                pltpu.VMEM((128, 256), BF16),
                pltpu.VMEM((128, 256), F32),
                pltpu.VMEM((128, 256), F32),
                pltpu.VMEM((128, 256), F32),
                pltpu.VMEM((8, 128, 128), F32),
                pltpu.VMEM((8, 128, 128), F32),
                pltpu.SemaphoreType.DMA((6,)),
                pltpu.SemaphoreType.REGULAR((5,)),
                pltpu.SemaphoreType.DMA((2, 2, 2)),
                pltpu.SemaphoreType.DMA((2, 2, 2)),
                pltpu.SemaphoreType.DMA((2, 2)),
                pltpu.SemaphoreType.DMA((2, 2)),
                pltpu.SemaphoreType.DMA((2, 4, 2)),
                pltpu.SemaphoreType.DMA((2, 4, 2)),
                pltpu.SemaphoreType.DMA((8, 3)),
                pltpu.SemaphoreType.DMA((8, 3)),
            ],
            compiler_params=pltpu.CompilerParams(
                collective_id=0,
                has_side_effects=True,
                vmem_limit_bytes=60 * 1024 * 1024,
            ),
        )(subspace, ritz, hams, connect, send_rows)

    return jax.shard_map(
        per_device,
        mesh=mesh,
        in_specs=(
            P("state", "mesh"),
            P("state", None),
            P("mesh", None, None),
            P("mesh", None),
            P("mesh", None, None),
        ),
        out_specs=P("state", "mesh"),
        check_vma=False,
    )
```
